32 devices in a mesh: row: 8 (over y, x, core), col: 4 (over z).
Axes of the slice: x: 2, y: 2, z: 4, core: 2. Of those that a mesh axis runs over, the one named last changes fastest.
Arguments:
- residual: bfloat16 [512, 16, 5120], P('row', None, 'col'), may hold values from -6 to 6
- positions: int32 [512], P('row'), may hold values from 0 to 15
- norm_gain: float32 [5120], P('col'), may hold values from 0.1 to 1.9
- w_gate: bfloat16 [5120, 16384], P('col', 'row'), may hold values from -0.078125 to 0.078125
- w_up: bfloat16 [5120, 16384], P('col', 'row'), may hold values from -0.078125 to 0.078125
- covariance: float32 [16384, 16384], P('row', 'col'), may hold values from -1 to 4, as said below
Outputs:
- factor: float32 [16384, 16384], P('row', 'col')
The draws below stay inside these ranges and needn't reach their ends.
Inputs may be any that keep to these rules, and one draw needn't show every extreme that they name: `covariance`: symmetric positive definite in the natural order of hidden units.
All inputs are finite; a program needn't handle non-finite values.
Results may differ from the reference program's by a relative error of at most 0.0041.
Values may be sent and summed in bfloat16 or wider, within the bound.
No kernel may reach another device: no remote copies, remote signals or barrier semaphores. Data moves between devices by JAX's collectives and lax.ppermute only.
A program may use at most 128 MiB of HBM per device.

```python
import math
import jax
import jax.numpy as jnp
from jax import lax

D = 5120
KW = 16384
TILE = 64
PANEL = 256
NPANEL = 2
LEN = 16
PROMPTS = 512
N_ROW = 8
N_COL = 4


def draw_covariance(key, part):
    amplitude = 1.1 / KW
    first_key = jax.random.fold_in(key, 11)
    second_key = jax.random.fold_in(key, 12)
    third_key = jax.random.fold_in(key, 13)
    factor_rank = max(PANEL, 64)
    noise_field = jax.random.uniform(first_key, (KW, KW), jnp.float32, -amplitude, amplitude)
    loadings = jax.random.normal(third_key, (KW, factor_rank), jnp.float32)
    symmetric = 0.5 * (noise_field + noise_field.T)
    correlated = jnp.dot(loadings, loadings.T, precision=lax.Precision.HIGHEST, preferred_element_type=jnp.float32) * (0.5 / factor_rank)
    diagonal = jnp.exp(jax.random.uniform(second_key, (KW,), jnp.float32, math.log(1.2), math.log(2.4)))
    diag_index = jnp.arange(KW)
    natural = (symmetric + correlated).at[diag_index, diag_index].add(diagonal)
    tile_rows = KW // (N_ROW * TILE)
    tile_cols = KW // (N_COL * TILE)
    return natural.reshape(tile_rows, N_ROW, TILE, tile_cols, N_COL, TILE).transpose(1, 0, 2, 4, 3, 5).reshape(KW, KW)


def set_ends(entries, stream_key, low, largest):
    dims = entries.shape
    place = [jax.random.randint(jax.random.fold_in(stream_key, axis), (), 0, dims[axis]) for axis in range(len(dims))]
    entries = entries.at[tuple(place)].set(low)
    longest = dims.index(max(dims))
    place[longest] = (place[longest] + 1) % dims[longest]
    return entries.at[tuple(place)].set(largest)


def block_scale(key, extent, shards, least, top_value):
    gain = 1.0
    for position, shards_of in shards:
        draws = jax.random.uniform(jax.random.fold_in(jax.random.fold_in(key, 6), position), (shards_of,), jnp.float32, least / len(shards), top_value / len(shards))
        gain = gain * jnp.repeat(jnp.exp(draws), extent[position] // shards_of).reshape((-1,) + (1,) * (len(extent) - 1 - position))
    return gain


def bell_draw(rng, dims, deviation, reach, cuts=(), kind=jnp.bfloat16):
    values = jax.random.normal(rng, dims, jnp.float32) * deviation
    if len(cuts) > 0:
        values = block_scale(rng, dims, cuts, -0.22, 0.18) * values
    return jnp.clip(values, min=-reach, max=reach).astype(kind)


def setup_inputs(seed: int = 0) -> dict:
    seeds = jax.random.split(jax.random.key(seed), 7)
    return {
        "residual": bell_draw(seeds[0], (PROMPTS, LEN, D), 1.0, 6.0, ((0, 8), (2, 4))),
        "positions": set_ends(jax.random.randint(seeds[1], (PROMPTS,), 0, LEN), jax.random.fold_in(seeds[1], 1), 0, LEN - 1).astype(jnp.int32),
        "norm_gain": jnp.clip(1.0 + 0.18 * jax.random.normal(seeds[2], (D,), jnp.float32), 0.1, 1.9),
        "w_gate": bell_draw(seeds[3], (D, KW), D ** -0.5, 0.078125, ((0, 4), (1, 8))),
        "w_up": bell_draw(seeds[4], (D, KW), D ** -0.5, 0.078125, ((0, 4), (1, 8))),
        "covariance": draw_covariance(jax.random.fold_in(seeds[6], 71), 0),
    }


EPSILON = 1e-06

def to_natural(stored):
    tile_rows = KW // (N_ROW * TILE)
    tile_cols = KW // (N_COL * TILE)
    return stored.reshape(N_ROW, tile_rows, TILE, N_COL, tile_cols, TILE).transpose(1, 0, 2, 4, 3, 5).reshape(KW, KW)

def to_stored(natural):
    tile_rows = KW // (N_ROW * TILE)
    tile_cols = KW // (N_COL * TILE)
    return natural.reshape(tile_rows, N_ROW, TILE, tile_cols, N_COL, TILE).transpose(1, 0, 2, 4, 3, 5).reshape(KW, KW)

def reference(residual, positions, norm_gain, w_gate, w_up, covariance):
    prompt_total = residual.shape[0]
    pick_index = jnp.broadcast_to(positions[:, None, None], (prompt_total, 1, D))
    subject = jnp.take_along_axis(residual, pick_index, axis=1)[:, 0, :].astype(jnp.float32)
    inverse_rms = lax.rsqrt(lax.optimization_barrier(jnp.mean(subject * subject, axis=1, keepdims=True)) + EPSILON)
    normed = (subject * inverse_rms * norm_gain[None, :]).astype(jnp.bfloat16)
    gate_total = jnp.dot(normed.astype(jnp.float32), w_gate.astype(jnp.float32), preferred_element_type=jnp.float32)
    up_total = jnp.dot(normed.astype(jnp.float32), w_up.astype(jnp.float32), preferred_element_type=jnp.float32)
    raw_keys = jax.nn.silu(gate_total) * up_total
    key_scale = lax.rsqrt(lax.optimization_barrier(jnp.mean(raw_keys * raw_keys, axis=1, keepdims=True)) + EPSILON)
    unit_keys = (raw_keys * key_scale).astype(jnp.bfloat16)
    keys_outer = lax.dot_general(unit_keys.astype(jnp.float32), unit_keys.astype(jnp.float32), (((0,), (0,)), ((), ())), preferred_element_type=jnp.float32)
    matrix = to_natural(covariance) + keys_outer * (1.0 / prompt_total)
    indices = jnp.arange(KW, dtype=jnp.int32)
    for number in range(NPANEL):
        panel_start = number * PANEL
        panel_cols = matrix[:, panel_start:panel_start + PANEL]
        diag_block = panel_cols[panel_start:panel_start + PANEL]
        lower_factor = jnp.linalg.cholesky(diag_block)
        solved = jax.scipy.linalg.solve_triangular(lower_factor, panel_cols.T, lower=True).T
        shifted = indices - panel_start
        within = (shifted >= 0) & (shifted < PANEL)
        from_lower = jnp.take(lower_factor, jnp.clip(shifted, 0, PANEL - 1).astype(jnp.int32), axis=0)
        panel_factor = jnp.where((shifted >= PANEL)[:, None], solved, jnp.where(within[:, None], from_lower, jnp.zeros_like(solved)))
        matrix = matrix - lax.dot_general(panel_factor.astype(jnp.float32), panel_factor.astype(jnp.float32), (((1,), (1,)), ((), ())), precision=lax.Precision.HIGHEST, preferred_element_type=jnp.float32)
        matrix = matrix.at[:, panel_start:panel_start + PANEL].set(panel_factor)
    result = jnp.where(indices[:, None] >= indices[None, :], matrix, jnp.zeros_like(matrix))
    return to_stored(result)
```

```python
import functools

import jax
import jax.numpy as jnp
from jax import lax
from jax.experimental import pallas as pl
from jax.experimental.pallas import tpu as pltpu
from jax.sharding import PartitionSpec as P

TILE = 64
PANEL = 256
NPANEL = 2
JW = PANEL * NPANEL
JT = JW // TILE
EPSILON = 1e-06
HIGHEST = lax.Precision.HIGHEST
F32 = jnp.float32
BF16 = jnp.bfloat16

VMEM_LIMIT = 60 * 1024 * 1024


def mm(a, b, ca, cb, precision=None):
    return lax.dot_general(
        a, b, (((ca,), (cb,)), ((), ())), precision=precision, preferred_element_type=F32
    )


def params():
    return pltpu.CompilerParams(vmem_limit_bytes=VMEM_LIMIT)


def vmem():
    return pl.BlockSpec(memory_space=pltpu.VMEM)


def smem():
    return pl.BlockSpec(memory_space=pltpu.SMEM)


def row_swap(x, k):
    n = lax.axis_size("row")
    return lax.ppermute(x, "row", [(a, a ^ k) for a in range(n)])


def row_gather(x):
    n = lax.axis_size("row")
    blocks = [None] * n
    blocks[0] = x
    for k in range(2, n, 2):
        blocks[k] = row_swap(x, k)
    for k in range(0, n, 2):
        blocks[k + 1] = row_swap(blocks[k], 1)
    return blocks


def col_gather(x):
    n = lax.axis_size("col")
    up, down = [], []
    u = d = x
    for s in range(1, n):
        u = lax.ppermute(u, "col", [(a, a + 1) for a in range(s - 1, n - 1)])
        d = lax.ppermute(d, "col", [(a, a - 1) for a in range(1, n - s + 1)])
        up.append(u)
        down.append(d)
    return [x] + up + down


def cyclic(pieces):
    n = lax.axis_size("col")
    rank = lax.axis_index("col")
    up, down = pieces[1:n], pieces[n:]
    return [pieces[0]] + [
        jnp.where(rank >= s, up[s - 1], down[n - s - 1]) for s in range(1, n)
    ]


def side_by_side_kernel(n, rank_ref, *refs):
    out_ref = refs[-1]
    width = refs[0].shape[1]
    z = rank_ref[0]

    def place(source, ref):
        out_ref[:, pl.ds(pl.multiple_of(source * width, width), width)] = ref[...]

    place(z, refs[0])
    for s in range(1, n):

        @pl.when(z >= s)
        def _():
            place(z - s, refs[s])

        @pl.when(z + s < n)
        def _():
            place(z + s, refs[n - 1 + s])


def side_by_side(pieces, col_rank):
    n = lax.axis_size("col")
    height, width = pieces[0].shape
    if width % 128:
        blocks = in_order(cyclic(pieces), "col", False)
        return blocks.transpose(1, 0, 2).reshape(height, n * width)
    return pl.pallas_call(
        functools.partial(side_by_side_kernel, n),
        in_specs=[smem()] + [vmem()] * len(pieces),
        out_specs=vmem(),
        out_shape=jax.ShapeDtypeStruct((height, n * width), pieces[0].dtype),
        compiler_params=params(),
        name="side_by_side",
    )(col_rank, *pieces)


def panel_kernel(cols_ref, rows_ref, cols_out, rows_out):
    cols_out[...] = cols_ref[:, : cols_out.shape[1]].astype(BF16)
    rows_out[...] = rows_ref[...].astype(BF16)


def panel_parts(covariance, n):
    height, width = covariance.shape
    panel = JW // n
    wide = max(panel, 128)
    return pl.pallas_call(
        panel_kernel,
        grid=(1,),
        in_specs=[
            pl.BlockSpec((height, wide), lambda i: (0, 0)),
            pl.BlockSpec((TILE, width), lambda i: (0, 0)),
        ],
        out_specs=[
            pl.BlockSpec((height, panel), lambda i: (0, 0)),
            pl.BlockSpec((TILE, width), lambda i: (0, 0)),
        ],
        out_shape=[
            jax.ShapeDtypeStruct((height, panel), BF16),
            jax.ShapeDtypeStruct((TILE, width), BF16),
        ],
        compiler_params=params(),
        name="panel_parts",
    )(covariance, covariance)


def in_order(blocks, axis_name, xor):
    n = len(blocks)
    rank = lax.axis_index(axis_name)
    out = jnp.zeros((n,) + blocks[0].shape, blocks[0].dtype)
    for s, block in enumerate(blocks):
        place = rank ^ s if xor else lax.rem(rank - s + n, n)
        out = lax.dynamic_update_slice(out, block[None], (place,) + (0,) * block.ndim)
    return out


def col_sum(x):
    n = lax.axis_size("col")
    total = x
    for s in range(1, n):
        total = total + lax.ppermute(x, "col", [(a, (a + s) % n) for a in range(n)])
    return total


def row_sum(x):
    n = lax.axis_size("row")
    total = x
    for k in range(2, n, 2):
        total = total + row_swap(x, k)
    return total + row_swap(total, 1)


def scatter_sums(parts):
    n = lax.axis_size("col")
    rank = lax.axis_index("col")

    def share(part, index):
        return lax.dynamic_index_in_dim(part, jnp.clip(index, 0, n - 1), 0, keepdims=False)

    ups, downs = [None] * len(parts), [None] * len(parts)
    for s in range(1, n):
        for i, part in enumerate(parts):
            u, d = share(part, n - s + rank), share(part, rank - n + s)
            if s > 1:
                u = u + ups[i].astype(F32)
                d = d + downs[i].astype(F32)
            u, d = u.astype(jnp.float16), d.astype(jnp.float16)
            ups[i] = lax.ppermute(u, "col", [(a, a + 1) for a in range(s)])
            downs[i] = lax.ppermute(d, "col", [(a, a - 1) for a in range(n - s, n)])
    return [
        share(part, rank) + u.astype(F32) + d.astype(F32)
        for part, u, d in zip(parts, ups, downs)
    ]


def as_column(row):
    wide = jnp.broadcast_to(row[0:1, :], (128, row.shape[1]))
    return wide.T[:, 0:1]


def as_rows(column):
    wide = jnp.broadcast_to(column, (column.shape[0], 128))
    return wide.T[0:8, :]


def regroup(full, n, out_ref, which):
    lane = lax.broadcasted_iota(jnp.int32, (full.shape[0], 128), 1)
    for z in range(n):
        first = full[:, z // 2 * 128 : z // 2 * 128 + 128]
        second = full[:, (z + n) // 2 * 128 : (z + n) // 2 * 128 + 128]
        if z % 2 == 0:
            pair = jnp.where(lane < 64, first, pltpu.roll(second, 64, 1))
        else:
            pair = jnp.where(lane < 64, pltpu.roll(first, 64, 1), second)
        out_ref[z, which] = pair


def first_partial_kernel(n, nrow, rank_ref, *refs):
    blocks = refs[:nrow]
    wg_ref, wu_ref, part_ref, x_ref = refs[nrow:]
    local = blocks[0].shape[0]
    r = rank_ref[0]

    @pl.when(pl.program_id(0) == 0)
    def _():
        for k in range(nrow):
            x_ref[pl.ds(pl.multiple_of((r ^ k) * local, local), local), :] = blocks[k][...]

    x = x_ref[...]
    regroup(mm(x, wg_ref[...], 1, 0), n, part_ref, 0)
    regroup(mm(x, wu_ref[...], 1, 0), n, part_ref, 1)


def next_partial_kernel(n, x_ref, wg_ref, wu_ref, part_ref):
    x = x_ref[...]
    regroup(mm(x, wg_ref[...], 1, 0), n, part_ref, 0)
    regroup(mm(x, wu_ref[...], 1, 0), n, part_ref, 1)


def partials(subjects, w_gate, w_up, rank, n, nrow, chunks):
    features, hidden = w_gate.shape
    local = subjects[0].shape[0]
    prompts = local * nrow
    group = 128 * n
    groups = hidden // group
    per = groups // chunks
    cost = pl.CostEstimate(
        flops=4 * prompts * features * group * per,
        bytes_accessed=4 * features * group * per,
        transcendentals=0,
    )

    def weight(first):
        return pl.BlockSpec((features, group), lambda q: (0, q + first))

    part_shape = jax.ShapeDtypeStruct((n, 2, prompts, 128 * per), F32)
    part_spec = pl.BlockSpec((n, 2, prompts, 128), lambda q: (0, 0, 0, q))
    x_shape = jax.ShapeDtypeStruct((prompts, features), BF16)
    part, x = pl.pallas_call(
        functools.partial(first_partial_kernel, n, nrow),
        grid=(per,),
        in_specs=[smem()] + [vmem()] * nrow + [weight(0), weight(0)],
        out_specs=[part_spec, vmem()],
        out_shape=[part_shape, x_shape],
        compiler_params=params(),
        cost_estimate=cost,
        name="partial_first",
    )(rank, *subjects, w_gate, w_up)
    parts = [part]
    for chunk in range(1, chunks):
        parts.append(
            pl.pallas_call(
                functools.partial(next_partial_kernel, n),
                grid=(per,),
                in_specs=[vmem(), weight(chunk * per), weight(chunk * per)],
                out_specs=part_spec,
                out_shape=part_shape,
                compiler_params=params(),
                cost_estimate=cost,
                name="partial_next",
            )(x, w_gate, w_up)
        )
    return parts


def keys_kernel(chunks, *refs):
    sums = refs[:chunks]
    keys_ref, turned_ref, squares_ref = refs[chunks:]
    total = None
    for i in range(chunks):
        wide = sums[i].shape[2]
        gate, up = sums[i][0], sums[i][1]
        raw = gate / (1.0 + jnp.exp(-gate)) * up
        keys_ref[:, i * wide : (i + 1) * wide] = raw.astype(BF16)
        turned_ref[i * wide : (i + 1) * wide, :] = raw.T.astype(BF16)
        part = jnp.sum(raw * raw, axis=1, keepdims=True)
        total = part if total is None else total + part
    squares_ref[...] = as_rows(total)


def make_keys(sums):
    chunks = len(sums)
    _, prompts, wide = sums[0].shape
    return pl.pallas_call(
        functools.partial(keys_kernel, chunks),
        in_specs=[vmem()] * chunks,
        out_specs=[vmem()] * 3,
        out_shape=[
            jax.ShapeDtypeStruct((prompts, chunks * wide), BF16),
            jax.ShapeDtypeStruct((chunks * wide, prompts), BF16),
            jax.ShapeDtypeStruct((8, prompts), F32),
        ],
        compiler_params=params(),
        name="keys",
    )(*sums)


def eliminate(value, offset, out_ref, step=4):
    size = value.shape[0]
    for first in range(0, size, step):
        top = first // 8 * 8
        active = value[top - (size - value.shape[0]) :, :]
        cols = [
            jnp.broadcast_to(active[:, offset + j : offset + j + 1], active.shape)
            for j in range(first, first + step)
        ]
        rows = [active[j - top : j - top + 1, :] for j in range(first, first + step)]
        update = None
        for i in range(step):
            at = first + i - top
            pivot = cols[i][at : at + 1, :]
            inverse = 1.0 / pivot
            out_ref[first + i : first + i + 1, :] = rows[i] * lax.rsqrt(pivot)
            scaled = cols[i] * inverse
            for k in range(i + 1, step):
                rows[k] = rows[k] - rows[i] * scaled[at + k - i : at + k - i + 1, :]
                cols[k] = cols[k] - scaled * cols[i][at + k - i : at + k - i + 1, :]
            term = scaled * rows[i]
            update = term if update is None else update + term
        value = active - update


def factor_kernel(prompts, keys, n, nrow, rank_ref, key_sums_ref, kj_ref, *refs):
    cjj = refs[:nrow]
    inv_ref, inv_t_ref, m_ref, w_ref, o_ref = refs[nrow:]
    r = rank_ref[0]
    scale = lax.rsqrt(as_column(key_sums_ref[...]) / keys + EPSILON)
    unit = (kj_ref[...].astype(F32) * scale).astype(BF16)
    gram = mm(unit, unit, 0, 0) * (1.0 / prompts)
    per = JT // n

    def natural(a):
        return jnp.concatenate(
            [
                a[(t % n * per + t // n) * TILE : (t % n * per + t // n + 1) * TILE, :]
                for t in range(JT)
            ],
            axis=0,
        )

    def stored(a):
        return jnp.concatenate(
            [a[(q % per * n + q // per) * TILE : (q % per * n + q // per + 1) * TILE, :] for q in range(JT)],
            axis=0,
        )

    for k in range(nrow):

        @pl.when((r ^ k) < JT)
        def _():
            at = pl.ds(pl.multiple_of((r ^ k) * TILE, TILE), TILE)
            w_ref[at, :] = cjj[k][...].astype(F32)

    mixed = natural(gram) + w_ref[...]
    m_ref[:, :JW] = natural(mixed.T)
    eye_row = lax.broadcasted_iota(jnp.int32, (JW, JW), 0)
    eye_col = lax.broadcasted_iota(jnp.int32, (JW, JW), 1)
    m_ref[:, JW:] = jnp.where(eye_row == eye_col, 1.0, 0.0)
    lane = lax.broadcasted_iota(jnp.int32, (64, 128), 1)
    sub = lax.broadcasted_iota(jnp.int32, (64, 128), 0)

    def block(k, carry):
        base = pl.multiple_of(k * 128, 128)
        for half in range(2):
            at = pl.ds(pl.multiple_of(base + 64 * half, 64), 64)
            corner = m_ref[at, pl.ds(base, 128)]
            if half == 0:
                eliminate(jnp.where(lane < 64, corner, jnp.where(lane - 64 == sub, 1.0, 0.0)), 0, o_ref)
                inverse = o_ref[:, 64:128]
            else:
                eliminate(jnp.where(lane >= 64, corner, jnp.where(lane == sub, 1.0, 0.0)), 64, o_ref)
                inverse = o_ref[:, 0:64]
            solved = mm(inverse, m_ref[at, :], 1, 0, HIGHEST)
            w_ref[at, :] = solved[:, JW:]
            m_ref[...] = m_ref[...] - mm(solved[:, :JW], solved, 0, 0, HIGHEST)
        return carry

    lax.fori_loop(0, JW // 128, block, 0)
    inv = jnp.where(eye_row >= eye_col, w_ref[...], 0.0)
    inv_ref[...] = inv.astype(BF16)
    inv_t_ref[...] = stored(inv.T).astype(BF16)


def make_factor(rank, key_sums, kj, cjj, hidden, n):
    prompts = kj.shape[0]
    shape = jax.ShapeDtypeStruct((JW, JW), BF16)
    return pl.pallas_call(
        functools.partial(factor_kernel, prompts, hidden, n, len(cjj)),
        in_specs=[smem()] + [vmem()] * (2 + len(cjj)),
        out_specs=[vmem()] * 2,
        out_shape=[shape, shape],
        scratch_shapes=[
            pltpu.VMEM((JW, 2 * JW), F32),
            pltpu.VMEM((JW, JW), F32),
            pltpu.VMEM((64, 128), F32),
        ],
        compiler_params=params(),
        name="factor",
    )(rank, key_sums, kj, *cjj)


def prepare_kernel(prompts, hidden, nrow, n, rank_ref, sums_ref, kj_ref, cjr_ref, *refs):
    turned = refs[: nrow // 2]
    keys = refs[nrow // 2 : nrow // 2 + nrow]
    cjc = refs[nrow // 2 + nrow : nrow // 2 + 2 * nrow]
    tk_ref, ar_ref, uk_ref, ac_ref, c_ref = refs[nrow // 2 + 2 * nrow :]
    r = rank_ref[0]
    per = JT // n
    scale = (1.0 / prompts) / (as_column(sums_ref[...]) / hidden + EPSILON)
    kj = kj_ref[...]
    kjs = (kj.astype(F32) * scale).astype(BF16)
    for k in range(nrow):
        source = r ^ k
        rows = turned[0].shape[1]
        at = pl.ds(pl.multiple_of(source * rows, rows), rows)
        piece = turned[k // 2][k % 2]
        tk_ref[at, :] = piece
        ar_ref[at, :] = (cjr_ref[at, :].astype(F32) + mm(piece, kjs, 1, 0)).astype(BF16)
    for k in range(nrow):
        source = r ^ k
        if nrow <= JT:
            c_ref[pl.ds(pl.multiple_of(source * TILE, TILE), TILE), :] = cjc[k][...]
        else:

            @pl.when(source < JT)
            def _():
                c_ref[pl.ds(pl.multiple_of(source * TILE, TILE), TILE), :] = cjc[k][...]

    for k in range(nrow):
        width = keys[0].shape[1]
        at = pl.ds(pl.multiple_of((r ^ k) * width, width), width)
        block = (keys[k][...].astype(F32) * scale).astype(BF16)
        uk_ref[:, at] = block
        cross = mm(kj, block, 0, 0)
        for t in range(JT):
            q = t % n * per + t // n
            rows = slice(t * TILE, (t + 1) * TILE)
            ac_ref[rows, at] = (
                c_ref[rows, at].astype(F32) + cross[q * TILE : (q + 1) * TILE, :]
            ).astype(BF16)


def prepare(rank, key_sums, kj, cjr, turned, keys, cjc, hidden, n):
    nrow = len(keys)
    prompts = kj.shape[0]
    rows = cjr.shape[0]
    cols = nrow * keys[0].shape[1]
    return pl.pallas_call(
        functools.partial(prepare_kernel, prompts, hidden, nrow, n),
        in_specs=[smem()] + [vmem()] * (3 + nrow // 2 + 2 * nrow),
        out_specs=[vmem()] * 4,
        out_shape=[
            jax.ShapeDtypeStruct((rows, prompts), BF16),
            jax.ShapeDtypeStruct((rows, JW), BF16),
            jax.ShapeDtypeStruct((prompts, cols), BF16),
            jax.ShapeDtypeStruct((JW, cols), BF16),
        ],
        scratch_shapes=[pltpu.VMEM((JW, cols), BF16)],
        compiler_params=params(),
        name="prepare",
    )(rank, key_sums, kj, cjr, *turned, *keys, *cjc)


def final_kernel(nrow, n, ranks_ref, tk_ref, ar_ref, uk_ref, ac_ref, inv_ref, inv_t_ref, c_ref, out_ref, tp_ref, up_ref, sel_ref):
    a, b = pl.program_id(0), pl.program_id(1)
    r, z = ranks_ref[0], ranks_ref[1]
    height, width = out_ref.shape
    panel = JW // n
    rows = pl.ds(pl.multiple_of(a * height, height), height)
    cols = pl.ds(pl.multiple_of(b * width, width), width)

    @pl.when((a == 0) & (b == 0))
    def _():
        k = lax.broadcasted_iota(jnp.int32, (JW, panel), 0)
        j = lax.broadcasted_iota(jnp.int32, (JW, panel), 1)
        hot = (k == (j // TILE * n + z) * TILE + j % TILE).astype(F32).astype(BF16)
        sel_ref[...] = mm(inv_t_ref[...], hot, 1, 0).astype(BF16)

    @pl.when(b == 0)
    def _():
        tp_ref[...] = mm(ar_ref[rows, :], inv_t_ref[...], 1, 0).astype(BF16)

    @pl.when(b == a)
    def _():
        up_ref[:, cols] = mm(inv_ref[...], ac_ref[:, cols], 1, 0).astype(BF16)

    @pl.when(b > a)
    def _():
        out_ref[...] = jnp.zeros_like(out_ref)

    def value():
        return (
            c_ref[...]
            + mm(tk_ref[rows, :], uk_ref[:, cols], 1, 0)
            - mm(tp_ref[...], up_ref[:, cols], 1, 0)
        )

    @pl.when(b < a)
    def _():
        out_ref[...] = value()

    def lower(shape):
        i = lax.broadcasted_iota(jnp.int32, shape, 0)
        j = lax.broadcasted_iota(jnp.int32, shape, 1)
        i_global = ((i // TILE + a * (height // TILE)) * nrow + r) * TILE + i % TILE
        j_global = ((j // TILE + b * (width // TILE)) * n + z) * TILE + j % TILE
        return i_global >= j_global

    @pl.when(b == a)
    def _():
        out_ref[...] = jnp.where(lower((height, width)), value(), 0.0)

    @pl.when(b == 0)
    def _():
        panel_rows = mm(ar_ref[rows, :], sel_ref[...], 1, 0)
        out_ref[:, :panel] = jnp.where((a > 0) | lower((height, panel)), panel_rows, 0.0)


def finish(ranks, tk, ar, uk, ac, inv, inv_t, covariance, nrow, n):
    row_count, col_count = covariance.shape
    blocks = 4
    height, width = row_count // blocks, col_count // blocks

    def whole(array):
        return pl.BlockSpec(array.shape, lambda a, b, s: (0, 0), pipeline_mode=pl.Buffered(1))

    block = (height, width)
    return pl.pallas_call(
        functools.partial(final_kernel, nrow, n),
        grid_spec=pltpu.PrefetchScalarGridSpec(
            num_scalar_prefetch=1,
            grid=(blocks, blocks),
            in_specs=[whole(x) for x in (tk, ar, uk, ac, inv, inv_t)]
            + [pl.BlockSpec(block, lambda a, b, s: (a, jnp.minimum(a, b)))],
            out_specs=pl.BlockSpec(block, lambda a, b, s: (a, b)),
            scratch_shapes=[
                pltpu.VMEM((height, JW), BF16),
                pltpu.VMEM((JW, col_count), BF16),
                pltpu.VMEM((JW, JW // n), BF16),
            ],
        ),
        out_shape=jax.ShapeDtypeStruct(covariance.shape, F32),
        compiler_params=params(),
        name="finish",
    )(ranks, tk, ar, uk, ac, inv, inv_t, covariance)


def on_device(residual, positions, norm_gain, w_gate, w_up, covariance):
    nrow, n = lax.axis_size("row"), lax.axis_size("col")
    r, z = lax.axis_index("row"), lax.axis_index("col")
    rank = jnp.reshape(r, (1,)).astype(jnp.int32)
    col_rank = jnp.reshape(z, (1,)).astype(jnp.int32)
    local_prompts, tokens, features = residual.shape
    hidden_local = w_gate.shape[1]
    hidden = hidden_local * nrow
    row_count, col_count = covariance.shape
    share_tiles = hidden_local // n // TILE
    sets = nrow // n
    per_set = share_tiles // sets

    token = lax.broadcasted_iota(jnp.int32, (local_prompts, tokens), 1)
    chosen = (token == positions[:, None])[:, :, None]
    subject = jnp.sum(jnp.where(chosen, residual, 0).astype(F32), axis=1)
    squares = col_sum(jnp.sum(subject * subject, axis=1))
    scale = lax.rsqrt(squares / (features * n) + EPSILON)[:, None]
    normed = row_gather((subject * scale * norm_gain[None, :]).astype(BF16))

    groups = hidden_local // (128 * n)
    chunks = 2 if groups % 2 == 0 else 1
    parts = partials(normed, w_gate, w_up, rank, n, nrow, chunks)

    panel_here, panel_rows = panel_parts(covariance, n)
    cjr = side_by_side(col_gather(panel_here), col_rank)
    cjc = row_gather(panel_rows)
    cjj = row_gather(cjr[:TILE, :])

    keys, turned, sums = make_keys(scatter_sums(parts))
    prompts = keys.shape[0]
    key_sums = row_sum(col_sum(sums))

    first = keys[:, : JW // n]
    up = [
        lax.ppermute(first, ("row", "col"), [(a, a + s) for a in range(n - s)])
        for s in range(1, n)
    ]
    down = [
        lax.ppermute(first, ("row", "col"), [(a, a - s) for a in range(s, n)])
        for s in range(1, n)
    ]
    kj = side_by_side([first] + up + down, col_rank)
    even = jnp.where(r == 0, kj, 0)
    for k in range(2, nrow, 2):
        even = even + lax.ppermute(kj, "row", [(0, k)])
    odd = lax.ppermute(even, "row", [(k, k + 1) for k in range(0, nrow, 2)])
    kj = jnp.where(r % 2 == 0, even, odd)

    col_keys = row_gather(keys)

    by_col = in_order(cyclic(col_gather(turned)), "col", False).reshape(
        n, per_set, sets, TILE, prompts
    )

    def piece(k):
        to = r ^ k
        got = lax.dynamic_slice(
            by_col,
            (lax.rem(to, n), 0, lax.div(to, n), 0, 0),
            (1, per_set, 1, TILE, prompts),
        )
        return got.reshape(per_set * TILE, prompts)

    across = row_swap(jnp.stack([piece(k) for k in range(1, nrow, 2)]), 1)
    row_keys = []
    for k in range(0, nrow, 2):
        pair = jnp.stack([piece(k), across[k // 2]])
        row_keys.append(pair if k == 0 else row_swap(pair, k))

    inv, inv_t = make_factor(rank, key_sums, kj, cjj, hidden, n)
    tk, ar, uk, ac = prepare(
        rank, key_sums, kj, cjr, row_keys, col_keys, cjc, hidden, n
    )
    ranks = jnp.concatenate([rank, col_rank])
    return finish(ranks, tk, ar, uk, ac, inv, inv_t, covariance, nrow, n)


def solution(mesh):
    placed = (
        P("row", None, "col"),
        P("row"),
        P("col"),
        P("col", "row"),
        P("col", "row"),
        P("row", "col"),
    )
    return jax.shard_map(
        on_device, mesh=mesh, in_specs=placed, out_specs=P("row", "col"), check_vma=False
    )
```
